32 devices in a mesh: grp: 16 (over z, y, core), sub: 2 (over x).
Axes of the slice: x: 2, y: 2, z: 4, core: 2. Of those that a mesh axis runs over, the one named last changes fastest.
Arguments:
- state_zero: float32 [352, 16807], P(('grp', 'sub')), as said below
- state_one: float32 [224, 7776], P(('grp', 'sub')), as said below
- state_two: float32 [224, 7776], P(('grp', 'sub')), as said below
- state_three: float32 [128, 3125], P(('grp', 'sub')), as said below
- intra_zero: float32 [8, 7, 7], replicated, may hold values from -0.75 to 0.75
- intra_one: float32 [8, 6, 6], replicated, may hold values from -0.875 to 0.875
- intra_two: float32 [8, 6, 6], replicated, may hold values from -0.875 to 0.875
- intra_three: float32 [8, 5, 5], replicated, may hold values from -1 to 1
- intersections: float32 [3, 8, 7, 7], replicated, may hold values from -2 to 2
- positions: float32 [3, 8, 7, 7], replicated, may hold values from -2 to 2
- coupling_pair: int32 [24], replicated, may hold values from 0 to 2
- coupling_mode: int32 [24], replicated, may hold values from 0 to 7
- coupling_strength: float32 [24], replicated, may hold values from -3 to 3
Outputs:
- stepped_zero: float32 [352, 16807], P(('grp', 'sub'))
- stepped_one: float32 [224, 7776], P(('grp', 'sub'))
- stepped_two: float32 [224, 7776], P(('grp', 'sub'))
- stepped_three: float32 [128, 3125], P(('grp', 'sub'))
- density_zero: float32 [8, 7, 7], replicated
- density_one: float32 [8, 6, 6], replicated
- density_two: float32 [8, 6, 6], replicated
- density_three: float32 [8, 5, 5], replicated
The draws below stay inside these ranges and needn't reach their ends.
Inputs may be any that keep to these rules, and one draw needn't show every extreme that they name: `state_zero`: rows from 7**3 on are zero. `state_one`: rows from 6**3 on are zero. `state_two`: rows from 6**3 on are zero. `state_three`: rows from 5**3 on are zero.
All inputs are finite; a program needn't handle non-finite values.
Results may differ from the reference program's by a relative error of at most 0.0001.
Values sent between devices are 32-bit elements; how exact they have to be, the bound alone decides.
A program may use at most 256 MiB of HBM per device.

```python
import math
import jax
import jax.numpy as jnp
from jax import lax

N0 = 7
N1 = 6
N2 = 6
N3 = 5
F = 8
PAIRS = 3
TERMS = 24
PAD0 = 352
PAD1 = 224
PAD2 = 224
PAD3 = 128


def state_draw(key, mode_width, rows_total):
    real_rows = mode_width ** 3
    columns = mode_width ** 5
    value_key, column_key = jax.random.split(key)
    row_pos = jnp.arange(rows_total).astype(jnp.float32)
    values = jax.random.normal(value_key, (rows_total, columns), jnp.float32)
    row_scale = 10.0 ** (row_pos / real_rows)
    divisor = 20.0
    live_rows = (row_pos < real_rows).astype(jnp.float32)
    tail_pos = (jnp.arange(columns) % real_rows).astype(jnp.float32)
    jitter = jax.random.uniform(column_key, (columns,), jnp.float32)
    column_scale = 10.0 ** (0.7 * tail_pos / real_rows + 0.3 * jitter)
    return values * (row_scale * live_rows)[:, None] * column_scale[None, :] / divisor


def draw_state_zero(key, part):
    return state_draw(jax.random.fold_in(key, 101), N0, PAD0)


def draw_state_one(key, part):
    return state_draw(jax.random.fold_in(key, 202), N1, PAD1)


def draw_state_two(key, part):
    return state_draw(jax.random.fold_in(key, 303), N2, PAD2)


def draw_state_three(key, part):
    return state_draw(jax.random.fold_in(key, 404), N3, PAD3)


def place_ends(entries, stream_key, low, largest):
    index_at = [jax.random.randint(jax.random.fold_in(stream_key, axis), (), 0, length) for axis, length in enumerate(entries.shape)]
    main_axis = entries.shape.index(max(entries.shape))
    neighbour = index_at[:main_axis] + [(index_at[main_axis] + 1) % entries.shape[main_axis]] + index_at[main_axis + 1:]
    return entries.at[tuple(index_at)].set(low).at[tuple(neighbour)].set(largest)


def scatter_about(own_key, extent, spread, limit, kind=jnp.bfloat16):
    entries = jax.random.normal(own_key, extent, jnp.float32) * spread
    return jnp.minimum(jnp.maximum(entries, -limit), limit).astype(kind)


def setup_inputs(seed: int = 0) -> dict:
    keys = jax.random.split(jax.random.key(seed), 14)
    return {
        "state_zero": draw_state_zero(jax.random.fold_in(keys[13], 71), 0),
        "state_one": draw_state_one(jax.random.fold_in(keys[13], 71), 0),
        "state_two": draw_state_two(jax.random.fold_in(keys[13], 71), 0),
        "state_three": draw_state_three(jax.random.fold_in(keys[13], 71), 0),
        "intra_zero": scatter_about(keys[4], (F, N0, N0), (F * N0) ** -0.5, 0.75, jnp.float32),
        "intra_one": scatter_about(keys[5], (F, N1, N1), (F * N1) ** -0.5, 0.875, jnp.float32),
        "intra_two": scatter_about(keys[6], (F, N2, N2), (F * N2) ** -0.5, 0.875, jnp.float32),
        "intra_three": scatter_about(keys[7], (F, N3, N3), (F * N3) ** -0.5, 1.0, jnp.float32),
        "intersections": scatter_about(keys[8], (PAIRS, F, N0, N0), N0 ** -0.5, 2.0, jnp.float32),
        "positions": scatter_about(keys[9], (PAIRS, F, N0, N0), N0 ** -0.5, 2.0, jnp.float32),
        "coupling_pair": place_ends(jax.random.randint(keys[10], (TERMS,), 0, PAIRS), jax.random.fold_in(keys[10], 1), 0, PAIRS - 1).astype(jnp.int32),
        "coupling_mode": place_ends(jax.random.randint(keys[11], (TERMS,), 0, F), jax.random.fold_in(keys[11], 1), 0, F - 1).astype(jnp.int32),
        "coupling_strength": scatter_about(keys[12], (TERMS,), 0.5, 3.0, jnp.float32),
    }


highest = lax.Precision.HIGHEST
time_step = 0.25


def along_mode(tensor, matrix, axis_at):
    old_shape = tensor.shape
    before = math.prod(old_shape[:axis_at])
    behind = math.prod(old_shape[axis_at + 1:])
    shaped = tensor.reshape(before, old_shape[axis_at], behind)
    result = jnp.einsum("ab,xby->xay", matrix, shaped, precision=highest)
    return result.reshape(old_shape[:axis_at] + (matrix.shape[0],) + old_shape[axis_at + 1:])


def coupled(source, over_mats, pos_mats, weights):
    zero_part = source
    one_part = None
    modes_count = source.ndim
    for axis_at in range(modes_count):
        moved_part = weights[axis_at] * along_mode(zero_part, pos_mats[axis_at], axis_at)
        if one_part is not None:
            moved_part = along_mode(one_part, over_mats[axis_at], axis_at) + moved_part
        if axis_at + 1 < modes_count:
            zero_part = along_mode(zero_part, over_mats[axis_at], axis_at)
        one_part = moved_part
    return one_part


def intra(tensor, operator_set):
    summed = jnp.zeros_like(tensor)
    for axis_at in range(tensor.ndim):
        summed = summed + along_mode(tensor, operator_set[axis_at], axis_at)
    return summed


def density(tensor):
    mode_width = tensor.shape[0]
    per_mode = []
    for axis_at in range(tensor.ndim):
        before = mode_width ** axis_at
        behind = mode_width ** (tensor.ndim - 1 - axis_at)
        shaped = tensor.reshape(before, mode_width, behind)
        per_mode.append(jnp.einsum("xiy,xjy->ij", shaped, shaped, precision=highest))
    return jnp.stack(per_mode) / float(mode_width ** (tensor.ndim - 1))


def reference(state_zero, state_one, state_two, state_three, intra_zero, intra_one, intra_two, intra_three, intersections, positions, coupling_pair, coupling_mode, coupling_strength):
    packed = [state_zero, state_one, state_two, state_three]
    operators = [intra_zero, intra_one, intra_two, intra_three]
    padded_rows = [PAD0, PAD1, PAD2, PAD3]
    widths = [N0, N1, N2, N3]
    tensors = []
    for state_index in range(4):
        span_rows = widths[state_index] ** 3
        tensors.append(packed[state_index][:span_rows].reshape((widths[state_index],) * F))
    pair_pick = (coupling_pair[:, None] == jnp.arange(PAIRS, dtype=jnp.int32)[None, :]).astype(coupling_strength.dtype)
    mode_pick = (coupling_mode[:, None] == jnp.arange(F, dtype=jnp.int32)[None, :]).astype(coupling_strength.dtype)
    weight_table = jnp.einsum("t,tp,tk->pk", coupling_strength, pair_pick, mode_pick, precision=highest)
    actions = [intra(tensors[state_index], operators[state_index]) for state_index in range(4)]
    for pair_index in range(PAIRS):
        lower_state = pair_index
        upper_state = pair_index + 1
        over_mats = intersections[pair_index, :, :widths[lower_state], :widths[upper_state]]
        pos_mats = positions[pair_index, :, :widths[lower_state], :widths[upper_state]]
        actions[lower_state] = actions[lower_state] + coupled(tensors[upper_state], over_mats, pos_mats, weight_table[pair_index])
        actions[upper_state] = actions[upper_state] + coupled(tensors[lower_state], jnp.transpose(over_mats, (0, 2, 1)), jnp.transpose(pos_mats, (0, 2, 1)), weight_table[pair_index])
    outputs = []
    densities = []
    for state_index in range(4):
        mode_width = widths[state_index]
        stepped = (tensors[state_index] - time_step * actions[state_index]).reshape(mode_width ** 3, mode_width ** (F - 3))
        filler = jnp.zeros((padded_rows[state_index] - mode_width ** 3, mode_width ** (F - 3)), stepped.dtype)
        outputs.append(jnp.concatenate([stepped, filler], axis=0))
        densities.append(density(tensors[state_index]))
    return (outputs[0], outputs[1], outputs[2], outputs[3], densities[0], densities[1], densities[2], densities[3])
```

```python
import functools
import math

import jax
import jax.numpy as jnp
import numpy as np
from jax import lax
from jax.experimental import pallas as pl
from jax.experimental.pallas import tpu as pltpu
from jax.sharding import PartitionSpec as P

highest = lax.Precision.HIGHEST
high = lax.Precision.HIGH
time_step = 0.25
lanes = 128
vmem_limit = 60 * 1024 * 1024
params = pltpu.CompilerParams(vmem_limit_bytes=vmem_limit)
vmem = pl.BlockSpec(memory_space=pltpu.VMEM)


def digits(width, count, total, place):
    index = np.arange(total)
    live = index < width**count
    digit = (index // width ** (count - 1 - place)) % width
    return ((digit[None, :] == np.arange(width)[:, None]) & live[None, :]).astype(np.float32)


def others(width, count, total, place):
    index = np.arange(total)
    stride = width ** (count - 1 - place)
    rest = index - ((index // stride) % width) * stride
    return np.where(index < width**count, rest, -1).astype(np.int32)


def split(value):
    top = value.astype(jnp.bfloat16)
    return top, (value - top.astype(jnp.float32)).astype(jnp.bfloat16)


def dot3(left, right, contract):
    dims = (contract, ((), ()))
    go = functools.partial(lax.dot_general, dimension_numbers=dims, preferred_element_type=jnp.float32)
    return go(left[0], right[0]) + (go(left[0], right[1]) + go(left[1], right[0]))


def pack_kernel(plan, *refs):
    sources, out = refs[:-1], refs[-1]
    row = 0
    for source, (rows, columns, tiles) in zip(sources, plan):
        for device in range(out.shape[0]):
            for tile in range(tiles):
                start = (device * tiles + tile) * lanes
                width = min(lanes, columns - start)
                at = slice(row + tile * rows, row + (tile + 1) * rows)
                if width < lanes:
                    out[device, at, :] = jnp.zeros((rows, lanes), jnp.float32)
                if width > 0:
                    out[device, at, :width] = source[:, start : start + width]
        row += tiles * rows


def build_kernel(jobs, *refs):
    count = len(jobs)
    inputs, outputs = refs[:count], refs[count:-2]
    inner_over, inner_pos = refs[-2:]
    at = 0
    for source, (width, modes, rows, keep) in zip(inputs, jobs):
        cols = source.shape[-1]
        over = [source[0, k] for k in range(modes)]
        pos = [source[1, k] for k in range(modes)]
        if keep:
            over_out, pos_out = outputs[at], outputs[at + 1]
            at += 2
        else:
            over_out, pos_out = None, outputs[at]
            at += 1
        real = width**modes
        if rows > real:
            for out in (over_out, pos_out):
                if out is not None:
                    out[real:, :] = jnp.zeros((rows - real, cols), jnp.float32)
        first, second = over[modes - 2], over[modes - 1]
        first_pos, second_pos = pos[modes - 2], pos[modes - 1]
        for a in range(width):
            span = slice(a * width, (a + 1) * width)
            over_value = first[a : a + 1] * second
            pos_value = first_pos[a : a + 1] * second + first[a : a + 1] * second_pos
            if modes == 2:
                pos_out[span, :] = pos_value
                if keep:
                    over_out[span, :] = over_value
            else:
                inner_over[span, :cols] = over_value
                inner_pos[span, :cols] = pos_value
        if modes == 3:
            square = width * width
            over_value = inner_over[:square, :cols]
            pos_value = inner_pos[:square, :cols]
            for a in range(width):
                span = slice(a * square, (a + 1) * square)
                pos_out[span, :] = pos[0][a : a + 1] * over_value + over[0][a : a + 1] * pos_value
                if keep:
                    over_out[span, :] = over[0][a : a + 1] * over_value


def mix_kernel(plan, arrived, *refs):
    matrix_count = sum(len(item[2]) for item in plan)
    matrices = refs[:matrix_count]
    out = refs[matrix_count]
    grams = refs[matrix_count + 1 : matrix_count + 1 + len(plan)]
    gathered, result = refs[-2:]
    devices = arrived.shape[0]
    row = 0
    out_row = 0
    at = 0
    for state, (rows, tiles, targets) in enumerate(plan):
        total, width = rows * devices, tiles * lanes
        for device in range(devices):
            for tile in range(tiles):
                start = row + tile * rows
                gathered[device * rows : (device + 1) * rows, tile * lanes : (tile + 1) * lanes] = arrived[
                    device, start : start + rows, :
                ]
        row += tiles * rows
        value = split(gathered[:total, :width])
        grams[state][...] = dot3(value, value, ((1,), (1,)))
        for target_rows in targets:
            target_total = target_rows * devices
            result[:target_total, :width] = dot3(split(matrices[at][...]), value, ((1,), (0,)))
            at += 1
            for device in range(devices):
                for tile in range(tiles):
                    start = out_row + tile * target_rows
                    out[device, start : start + target_rows, :] = result[
                        device * target_rows : (device + 1) * target_rows, tile * lanes : (tile + 1) * lanes
                    ]
            out_row += target_rows * tiles


def unpack_kernel(plan, returned, *refs):
    devices = returned.shape[0]
    row = 0
    at = 0
    for rows_list, columns, tiles in plan:
        action, rest = refs[at], refs[at + 1]
        at += 2
        rest_row = 0
        for position, rows in enumerate(rows_list):
            for device in range(devices):
                for tile in range(tiles):
                    start = (device * tiles + tile) * lanes
                    width = min(lanes, columns - start)
                    if width > 0:
                        value = returned[device, row + tile * rows : row + (tile + 1) * rows, :width]
                        if position == 0:
                            action[:, start : start + width] = value
                        else:
                            rest[rest_row : rest_row + rows, start : start + width] = value
            row += rows * tiles
            if position:
                rest_row += rows


def density_kernel(jobs, *refs):
    out = refs[-1]
    out[...] = jnp.zeros_like(out)
    at = 0
    for modes in jobs:
        gram = refs[at][...]
        for state_mode, width in modes:
            rest_rows, rest_columns, pick = refs[at + 1], refs[at + 2], refs[at + 3]
            k = state_mode[1]
            place = state_mode[2]
            kept = jnp.where(rest_rows[:, place : place + 1] == rest_columns[place : place + 1, :], gram, 0.0)
            left = jnp.dot(pick[place], kept, precision=highest, preferred_element_type=jnp.float32)
            value = lax.dot_general(
                left, pick[place], (((1,), (1,)), ((), ())), precision=highest, preferred_element_type=jnp.float32
            )
            out[state_mode[0] * 8 + k, :, :] = value
        at += 4


def call(kernel, outs, scratch, *args, name):
    return pl.pallas_call(
        kernel,
        out_shape=[jax.ShapeDtypeStruct(shape, jnp.float32) for shape in outs],
        in_specs=[vmem] * len(args),
        out_specs=[vmem] * len(outs),
        scratch_shapes=[pltpu.VMEM(shape, jnp.float32) for shape in scratch],
        compiler_params=params,
        name=name,
    )(*args)


def round_up(value, unit):
    return -(-value // unit) * unit


def exchange(blocks):
    return lax.all_to_all(blocks, ("grp", "sub"), split_axis=0, concat_axis=0, tiled=True)


def local(*args):
    states = args[:4]
    operators = args[4:8]
    intersections, positions, coupling_pair, coupling_mode, coupling_strength = args[8:]
    devices = lax.axis_size("grp") * lax.axis_size("sub")
    count = len(states)
    widths = [operator.shape[1] for operator in operators]
    rows = [state.shape[0] for state in states]
    columns = [state.shape[1] for state in states]
    totals = [size * devices for size in rows]
    tiles = [-(-size // (devices * lanes)) for size in columns]
    pairs, modes = intersections.shape[:2]

    sent_rows = sum(rows[s] * tiles[s] for s in range(count))
    (sends,) = call(
        functools.partial(pack_kernel, [(rows[s], columns[s], tiles[s]) for s in range(count)]),
        [(devices, sent_rows, lanes)],
        [],
        *states,
        name="pack",
    )
    arrived = exchange(sends)

    pair_pick = (coupling_pair[:, None] == jnp.arange(pairs, dtype=jnp.int32)[None, :]).astype(jnp.float32)
    mode_pick = (coupling_mode[:, None] == jnp.arange(modes, dtype=jnp.int32)[None, :]).astype(jnp.float32)
    weight_table = jnp.sum(
        coupling_strength[:, None, None] * pair_pick[:, :, None] * mode_pick[:, None, :], axis=0
    )
    both = jnp.stack([intersections, weight_table[:, :, None, None] * positions])

    small = {}
    for p in range(pairs):
        cut = both[:, p, :, : widths[p], : widths[p + 1]]
        small[(p, p + 1)] = cut
        small[(p + 1, p)] = jnp.swapaxes(cut, 2, 3)
    for s in range(count):
        unit = jnp.broadcast_to(jnp.eye(widths[s], dtype=jnp.float32), operators[s].shape)
        small[(s, s)] = jnp.stack([unit, operators[s]])
    jobs = []
    expanded = []
    shapes = []
    names = []
    for s, t in small:
        keep = s != t
        for part, at, span, row_total, column_total in (
            ("lead", 0, 3, totals[s], totals[t]),
            ("middle", 3, 2, widths[s] ** 2, widths[t] ** 2),
            ("tail", 5, 3, widths[s] ** 3, widths[t] ** 3),
        ):
            pick = np.stack([digits(widths[t], span, column_total, place) for place in range(span)])
            expanded.append(
                jnp.einsum("mkab,kbc->mkac", small[(s, t)][:, at : at + span], jnp.asarray(pick), precision=highest)
            )
            jobs.append((widths[s], span, row_total, keep))
            for kind in ("over", "pos") if keep else ("pos",):
                shapes.append((row_total, column_total))
                names.append((s, t, part, kind))
    widest = round_up(max(max(totals), max(widths) ** 3), lanes)
    built = call(
        functools.partial(build_kernel, jobs),
        shapes,
        [(round_up(max(widths) ** 2, 8), widest)] * 2,
        *expanded,
        name="build",
    )
    matrices = dict(zip(names, built))

    order = [[(t, "pos")] + [(s, kind) for s in (t - 1, t + 1) if 0 <= s < count for kind in ("over", "pos")] for t in range(count)]
    return_rows = sum(rows[s] * tiles[t] for t in range(count) for s, kind in order[t])
    mixed = call(
        functools.partial(
            mix_kernel, [(rows[t], tiles[t], [rows[s] for s, kind in order[t]]) for t in range(count)]
        ),
        [(devices, return_rows, lanes)] + [(totals[t], totals[t]) for t in range(count)],
        [(max(totals), max(tiles) * lanes)] * 2,
        arrived,
        *[matrices[(s, t, "lead", kind)] for t in range(count) for s, kind in order[t]],
        name="mix",
    )
    returned = exchange(mixed[0])

    cubes = [states[t].reshape(rows[t], widths[t] ** 2, widths[t] ** 3) for t in range(count)]
    density_jobs = []
    density_args = []
    for t in range(count):
        middle = jnp.einsum("rqc,rpc->qp", cubes[t], cubes[t], precision=high)
        tail = jnp.einsum("rqc,rqd->cd", cubes[t], cubes[t], precision=high)
        for gram, at, span in ((mixed[1 + t], 0, 3), (middle, 3, 2), (tail, 5, 3)):
            size = gram.shape[0]
            rest = np.stack([others(widths[t], span, size, place) for place in range(span)])
            pick = np.zeros((span, 8, size), np.float32)
            for place in range(span):
                pick[place, : widths[t]] = digits(widths[t], span, size, place)
            density_jobs.append([((t, at + place, place), widths[t]) for place in range(span)])
            density_args += [gram, jnp.asarray(rest.T), jnp.asarray(rest), jnp.asarray(pick)]
    (blocks,) = call(
        functools.partial(density_kernel, density_jobs), [(count * 8, 8, 8)], [], *density_args, name="density"
    )
    summed = lax.psum(blocks, ("grp", "sub"))
    densities = [
        summed[t * 8 : t * 8 + modes, : widths[t], : widths[t]] / float(widths[t] ** (modes - 1)) for t in range(count)
    ]

    rest_rows = [sum(rows[s] for s, kind in order[t][1:]) for t in range(count)]
    unpacked = call(
        functools.partial(
            unpack_kernel, [([rows[s] for s, kind in order[t]], columns[t], tiles[t]) for t in range(count)]
        ),
        [shape for t in range(count) for shape in ((rows[t], columns[t]), (rest_rows[t], columns[t]))],
        [],
        returned,
        name="unpack",
    )
    right = functools.partial(jnp.einsum, "rqc,dc->rqd", precision=high)
    left = functools.partial(jnp.einsum, "aq,rqd->rad", precision=high)
    total = []
    for t in range(count):
        total.append(right(cubes[t], matrices[(t, t, "tail", "pos")]) + left(matrices[(t, t, "middle", "pos")], cubes[t]))
    for t in range(count):
        rest = unpacked[2 * t + 1].reshape(rest_rows[t], widths[t] ** 2, widths[t] ** 3)
        start = 0
        for s in (t - 1, t + 1):
            if not 0 <= s < count:
                continue
            over_rows = rest[start : start + rows[s]]
            pos_rows = rest[start + rows[s] : start + 2 * rows[s]]
            start += 2 * rows[s]
            over_tail, pos_tail = matrices[(s, t, "tail", "over")], matrices[(s, t, "tail", "pos")]
            once = right(pos_rows, over_tail) + right(over_rows, pos_tail)
            twice = right(over_rows, over_tail)
            total[s] = (
                total[s]
                + left(matrices[(s, t, "middle", "over")], once)
                + left(matrices[(s, t, "middle", "pos")], twice)
            )
    stepped = [
        states[s] - time_step * (total[s].reshape(rows[s], columns[s]) + unpacked[2 * s]) for s in range(count)
    ]
    return tuple(stepped) + tuple(densities)


def solution(mesh):
    spread = P(("grp", "sub"), None)
    return jax.shard_map(
        local,
        mesh=mesh,
        in_specs=(spread,) * 4 + (P(),) * 9,
        out_specs=(spread,) * 4 + (P(),) * 4,
        check_vma=False,
    )
```

```python
import functools
import math

import jax
import jax.numpy as jnp
import numpy as np
from jax import lax
from jax.experimental import pallas as pl
from jax.experimental.pallas import tpu as pltpu
from jax.sharding import PartitionSpec as P

highest = lax.Precision.HIGHEST
high = lax.Precision.HIGH
time_step = 0.25
lanes = 128
vmem_limit = 60 * 1024 * 1024
params = pltpu.CompilerParams(vmem_limit_bytes=vmem_limit)
vmem = pl.BlockSpec(memory_space=pltpu.VMEM)


def digits(width, count, total, place):
    index = np.arange(total)
    live = index < width**count
    digit = (index // width ** (count - 1 - place)) % width
    return ((digit[None, :] == np.arange(width)[:, None]) & live[None, :]).astype(np.float32)


def others(width, count, total, place):
    index = np.arange(total)
    stride = width ** (count - 1 - place)
    rest = index - ((index // stride) % width) * stride
    return np.where(index < width**count, rest, -1).astype(np.int32)


def split(value):
    top = value.astype(jnp.bfloat16)
    return top, (value - top.astype(jnp.float32)).astype(jnp.bfloat16)


def dot3(left, right, contract):
    dims = (contract, ((), ()))
    go = functools.partial(lax.dot_general, dimension_numbers=dims, preferred_element_type=jnp.float32)
    return go(left[0], right[0]) + (go(left[0], right[1]) + go(left[1], right[0]))


def pack_kernel(plan, *refs):
    sources, out = refs[:-1], refs[-1]
    row = 0
    for source, (rows, columns, tiles) in zip(sources, plan):
        for device in range(out.shape[0]):
            for tile in range(tiles):
                start = (device * tiles + tile) * lanes
                width = min(lanes, columns - start)
                at = slice(row + tile * rows, row + (tile + 1) * rows)
                if width < lanes:
                    out[device, at, :] = jnp.zeros((rows, lanes), jnp.float32)
                if width > 0:
                    out[device, at, :width] = source[:, start : start + width]
        row += tiles * rows


def build_kernel(jobs, *refs):
    count = len(jobs)
    inputs, outputs = refs[:count], refs[count:-2]
    inner_over, inner_pos = refs[-2:]
    at = 0
    for source, (width, modes, rows, keep) in zip(inputs, jobs):
        cols = source.shape[-1]
        over = [source[0, k] for k in range(modes)]
        pos = [source[1, k] for k in range(modes)]
        if keep:
            over_out, pos_out = outputs[at], outputs[at + 1]
            at += 2
        else:
            over_out, pos_out = None, outputs[at]
            at += 1
        real = width**modes
        if rows > real:
            for out in (over_out, pos_out):
                if out is not None:
                    out[real:, :] = jnp.zeros((rows - real, cols), jnp.float32)
        first, second = over[modes - 2], over[modes - 1]
        first_pos, second_pos = pos[modes - 2], pos[modes - 1]
        for a in range(width):
            span = slice(a * width, (a + 1) * width)
            over_value = first[a : a + 1] * second
            pos_value = first_pos[a : a + 1] * second + first[a : a + 1] * second_pos
            if modes == 2:
                pos_out[span, :] = pos_value
                if keep:
                    over_out[span, :] = over_value
            else:
                inner_over[span, :cols] = over_value
                inner_pos[span, :cols] = pos_value
        if modes == 3:
            square = width * width
            over_value = inner_over[:square, :cols]
            pos_value = inner_pos[:square, :cols]
            for a in range(width):
                span = slice(a * square, (a + 1) * square)
                pos_out[span, :] = pos[0][a : a + 1] * over_value + over[0][a : a + 1] * pos_value
                if keep:
                    over_out[span, :] = over[0][a : a + 1] * over_value


def mix_kernel(plan, arrived, *refs):
    matrix_count = sum(len(item[2]) for item in plan)
    matrices = refs[:matrix_count]
    outs = refs[matrix_count : -2 - len(plan)]
    grams = refs[-2 - len(plan) : -2]
    gathered, result = refs[-2:]
    devices = arrived.shape[0]
    row = 0
    out_rows = [0] * len(outs)
    at = 0
    for state, (rows, tiles, targets, group) in enumerate(plan):
        total, width = rows * devices, tiles * lanes
        for device in range(devices):
            for tile in range(tiles):
                start = row + tile * rows
                gathered[device * rows : (device + 1) * rows, tile * lanes : (tile + 1) * lanes] = arrived[
                    device, start : start + rows, :
                ]
        row += tiles * rows
        value = split(gathered[:total, :width])
        grams[state][...] = dot3(value, value, ((1,), (1,)))
        for target_rows in targets:
            target_total = target_rows * devices
            result[:target_total, :width] = dot3(split(matrices[at][...]), value, ((1,), (0,)))
            at += 1
            for device in range(devices):
                for tile in range(tiles):
                    start = out_rows[group] + tile * target_rows
                    outs[group][device, start : start + target_rows, :] = result[
                        device * target_rows : (device + 1) * target_rows, tile * lanes : (tile + 1) * lanes
                    ]
            out_rows[group] += target_rows * tiles


def unpack_kernel(plan, returned, *refs):
    devices = returned.shape[0]
    row = 0
    at = 0
    for rows_list, columns, tiles in plan:
        action, rest = refs[at], refs[at + 1]
        at += 2
        rest_row = 0
        for position, rows in enumerate(rows_list):
            for device in range(devices):
                for tile in range(tiles):
                    start = (device * tiles + tile) * lanes
                    width = min(lanes, columns - start)
                    if width > 0:
                        value = returned[device, row + tile * rows : row + (tile + 1) * rows, :width]
                        if position == 0:
                            action[:, start : start + width] = value
                        else:
                            rest[rest_row : rest_row + rows, start : start + width] = value
            row += rows * tiles
            if position:
                rest_row += rows


def density_kernel(jobs, *refs):
    out = refs[-1]
    out[...] = jnp.zeros_like(out)
    at = 0
    for modes in jobs:
        gram = refs[at][...]
        for state_mode, width in modes:
            rest_rows, rest_columns, pick = refs[at + 1], refs[at + 2], refs[at + 3]
            k = state_mode[1]
            place = state_mode[2]
            kept = jnp.where(rest_rows[:, place : place + 1] == rest_columns[place : place + 1, :], gram, 0.0)
            left = jnp.dot(pick[place], kept, precision=highest, preferred_element_type=jnp.float32)
            value = lax.dot_general(
                left, pick[place], (((1,), (1,)), ((), ())), precision=highest, preferred_element_type=jnp.float32
            )
            out[state_mode[0] * 8 + k, :, :] = value
        at += 4


def call(kernel, outs, scratch, *args, name, cost=None):
    return pl.pallas_call(
        kernel,
        out_shape=[jax.ShapeDtypeStruct(shape, jnp.float32) for shape in outs],
        in_specs=[vmem] * len(args),
        out_specs=[vmem] * len(outs),
        scratch_shapes=[pltpu.VMEM(shape, jnp.float32) for shape in scratch],
        compiler_params=params,
        cost_estimate=cost,
        name=name,
    )(*args)


def round_up(value, unit):
    return -(-value // unit) * unit


def exchange(blocks):
    return lax.all_to_all(blocks, ("grp", "sub"), split_axis=0, concat_axis=0, tiled=True)


def local(*args):
    states = args[:4]
    operators = args[4:8]
    intersections, positions, coupling_pair, coupling_mode, coupling_strength = args[8:]
    devices = lax.axis_size("grp") * lax.axis_size("sub")
    count = len(states)
    widths = [operator.shape[1] for operator in operators]
    rows = [state.shape[0] for state in states]
    columns = [state.shape[1] for state in states]
    totals = [size * devices for size in rows]
    tiles = [-(-size // (devices * lanes)) for size in columns]
    pairs, modes = intersections.shape[:2]

    sent_rows = sum(rows[s] * tiles[s] for s in range(count))
    (sends,) = call(
        functools.partial(pack_kernel, [(rows[s], columns[s], tiles[s]) for s in range(count)]),
        [(devices, sent_rows, lanes)],
        [],
        *states,
        name="pack",
    )
    arrived = exchange(sends)

    pair_pick = (coupling_pair[:, None] == jnp.arange(pairs, dtype=jnp.int32)[None, :]).astype(jnp.float32)
    mode_pick = (coupling_mode[:, None] == jnp.arange(modes, dtype=jnp.int32)[None, :]).astype(jnp.float32)
    weight_table = jnp.sum(
        coupling_strength[:, None, None] * pair_pick[:, :, None] * mode_pick[:, None, :], axis=0
    )
    both = jnp.stack([intersections, weight_table[:, :, None, None] * positions])

    small = {}
    for p in range(pairs):
        cut = both[:, p, :, : widths[p], : widths[p + 1]]
        small[(p, p + 1)] = cut
        small[(p + 1, p)] = jnp.swapaxes(cut, 2, 3)
    for s in range(count):
        unit = jnp.broadcast_to(jnp.eye(widths[s], dtype=jnp.float32), operators[s].shape)
        small[(s, s)] = jnp.stack([unit, operators[s]])
    jobs = []
    expanded = []
    shapes = []
    names = []
    for s, t in small:
        keep = s != t
        for part, at, span, row_total, column_total in (
            ("lead", 0, 3, totals[s], totals[t]),
            ("middle", 3, 2, widths[s] ** 2, widths[t] ** 2),
            ("tail", 5, 3, widths[s] ** 3, widths[t] ** 3),
        ):
            pick = np.stack([digits(widths[t], span, column_total, place) for place in range(span)])
            expanded.append(
                jnp.einsum("mkab,kbc->mkac", small[(s, t)][:, at : at + span], jnp.asarray(pick), precision=highest)
            )
            jobs.append((widths[s], span, row_total, keep))
            for kind in ("over", "pos") if keep else ("pos",):
                shapes.append((row_total, column_total))
                names.append((s, t, part, kind))
    widest = round_up(max(max(totals), max(widths) ** 3), lanes)
    built = call(
        functools.partial(build_kernel, jobs),
        shapes,
        [(round_up(max(widths) ** 2, 8), widest)] * 2,
        *expanded,
        name="build",
    )
    matrices = dict(zip(names, built))

    order = [[(t, "pos")] + [(s, kind) for s in (t - 1, t + 1) if 0 <= s < count for kind in ("over", "pos")] for t in range(count)]
    groups = [list(range(1, count)), [0]]
    group_of = {t: g for g, members in enumerate(groups) for t in members}
    return_rows = [sum(rows[s] * tiles[t] for t in members for s, kind in order[t]) for members in groups]
    mixed = call(
        functools.partial(
            mix_kernel,
            [(rows[t], tiles[t], [rows[s] for s, kind in order[t]], group_of[t]) for t in range(count)],
        ),
        [(devices, size, lanes) for size in return_rows] + [(totals[t], totals[t]) for t in range(count)],
        [(max(totals), max(tiles) * lanes)] * 2,
        arrived,
        *[matrices[(s, t, "lead", kind)] for t in range(count) for s, kind in order[t]],
        name="mix",
    )

    cubes = [states[t].reshape(rows[t], widths[t] ** 2, widths[t] ** 3) for t in range(count)]
    density_jobs = []
    density_args = []
    for t in range(count):
        middle = jnp.einsum("rqc,rpc->qp", cubes[t], cubes[t], precision=high)
        tail = jnp.einsum("rqc,rqd->cd", cubes[t], cubes[t], precision=high)
        for gram, at, span in ((mixed[len(groups) + t], 0, 3), (middle, 3, 2), (tail, 5, 3)):
            size = gram.shape[0]
            rest = np.stack([others(widths[t], span, size, place) for place in range(span)])
            pick = np.zeros((span, 8, size), np.float32)
            for place in range(span):
                pick[place, : widths[t]] = digits(widths[t], span, size, place)
            density_jobs.append([((t, at + place, place), widths[t]) for place in range(span)])
            density_args += [gram, jnp.asarray(rest.T), jnp.asarray(rest), jnp.asarray(pick)]
    (blocks,) = call(
        functools.partial(density_kernel, density_jobs), [(count * 8, 8, 8)], [], *density_args, name="density",
        cost=pl.CostEstimate(flops=2 * 10**9, bytes_accessed=4 * 10**7, transcendentals=0),
    )
    flat = blocks.reshape(-1, lanes)
    copies = jnp.broadcast_to(flat, (devices,) + flat.shape)
    returned = [exchange(mixed[0]), exchange(jnp.concatenate([mixed[1], copies], axis=1))]
    summed = jnp.sum(returned[1][:, return_rows[1] :], axis=0).reshape(blocks.shape)
    densities = [
        summed[t * 8 : t * 8 + modes, : widths[t], : widths[t]] / float(widths[t] ** (modes - 1)) for t in range(count)
    ]

    rest_rows = [sum(rows[s] for s, kind in order[t][1:]) for t in range(count)]
    unpacked = {}
    for g, members in enumerate(groups):
        pieces = call(
            functools.partial(
                unpack_kernel, [([rows[s] for s, kind in order[t]], columns[t], tiles[t]) for t in members]
            ),
            [shape for t in members for shape in ((rows[t], columns[t]), (rest_rows[t], columns[t]))],
            [],
            returned[g],
            name="unpack",
        )
        for position, t in enumerate(members):
            unpacked[2 * t], unpacked[2 * t + 1] = pieces[2 * position], pieces[2 * position + 1]
    right = functools.partial(jnp.einsum, "rqc,dc->rqd", precision=high)
    left = functools.partial(jnp.einsum, "aq,rqd->rad", precision=high)
    total = []
    for t in range(count):
        total.append(right(cubes[t], matrices[(t, t, "tail", "pos")]) + left(matrices[(t, t, "middle", "pos")], cubes[t]))
    for t in list(range(1, count)) + [0]:
        rest = unpacked[2 * t + 1].reshape(rest_rows[t], widths[t] ** 2, widths[t] ** 3)
        start = 0
        for s in (t - 1, t + 1):
            if not 0 <= s < count:
                continue
            over_rows = rest[start : start + rows[s]]
            pos_rows = rest[start + rows[s] : start + 2 * rows[s]]
            start += 2 * rows[s]
            over_tail, pos_tail = matrices[(s, t, "tail", "over")], matrices[(s, t, "tail", "pos")]
            once = right(pos_rows, over_tail) + right(over_rows, pos_tail)
            twice = right(over_rows, over_tail)
            total[s] = (
                total[s]
                + left(matrices[(s, t, "middle", "over")], once)
                + left(matrices[(s, t, "middle", "pos")], twice)
            )
    stepped = [
        states[s] - time_step * (total[s].reshape(rows[s], columns[s]) + unpacked[2 * s]) for s in range(count)
    ]
    return tuple(stepped) + tuple(densities)


def solution(mesh):
    spread = P(("grp", "sub"), None)
    return jax.shard_map(
        local,
        mesh=mesh,
        in_specs=(spread,) * 4 + (P(),) * 9,
        out_specs=(spread,) * 4 + (P(),) * 4,
        check_vma=False,
    )
```
